512 devices in a mesh: expert: 16 (over x, y), tensor: 32 (over z, core).
Axes of the slice: x: 4, y: 4, z: 16, core: 2. Of those that a mesh axis runs over, the one named last changes fastest.
Arguments:
- tokens: bfloat16 [1024, 4096], P('expert', 'tensor'), may hold values from -6 to 6
- routes: int32 [1024, 2], P('expert'), may hold values from 0 to 7, all different within a row; in each aligned block of 64 rows (0 to 63, 64 to 127, ...) at most 32 rows name the same one
- route_weight: float32 [1024, 2], P('expert'), may hold values from 0.25 to 1
- gate_weight: bfloat16 [16, 5504, 4096], P('expert', 'tensor'), may hold values from -0.09375 to 0.09375
- up_weight: bfloat16 [16, 5504, 4096], P('expert', 'tensor'), may hold values from -0.09375 to 0.09375
- down_weight: bfloat16 [16, 5504, 4096], P('expert', 'tensor'), may hold values from -0.109375 to 0.109375
Outputs:
- mixed: bfloat16 [1024, 4096], P('expert', 'tensor')
The draws below stay inside these ranges and needn't reach their ends.
Inputs may be any that keep to these rules, and one draw needn't show every extreme that they name: `routes`: each row names two different experts; within the 64 rows of one index of expert no expert is named more than 32 times, a bound that some block reaches.
All inputs are finite; a program needn't handle non-finite values.
Results may differ from the reference program's by a relative error of at most 0.024.
Values may be sent and summed in bfloat16 or wider, within the bound.
No kernel may reach another device: no remote copies, remote signals or barrier semaphores. Data moves between devices by JAX's collectives and lax.ppermute only.
A program may use at most 64 MiB of HBM per device.

```python
import math
import jax
import jax.numpy as jnp
import numpy as np
from jax import lax

D = 4096
FF = 11008
TOK_DEV = 64
EXPERTS = 8
CAP = 32
TOKENS = 1024
N_EXPERT = 16
N_TENSOR = 32


def spiked(entries, own_key, source, target, blocks, factor):
    def block_of(position):
        return (jnp.arange(entries.shape[position]) // (entries.shape[position] // blocks)).reshape((-1,) + (1,) * (entries.ndim - 1 - position))

    near = jax.random.permutation(own_key, blocks)[block_of(target)]
    far = (block_of(target) + blocks // 2) % blocks
    return jnp.where((block_of(source) == near) | (block_of(source) == far), factor * entries, entries)


def level_of(rng, shape, shards, smallest, largest):
    def one(position, parts):
        heights = jax.random.uniform(jax.random.fold_in(jax.random.fold_in(rng, 6), position), (parts,), jnp.float32, smallest / len(shards), largest / len(shards))
        return jnp.repeat(jnp.exp(heights), shape[position] // parts).reshape((-1,) + (1,) * (len(shape) - position - 1))

    gain = one(*shards[0])
    for cut in shards[1:]:
        gain = gain * one(*cut)
    return gain


def routed_block(key, own, number, rows, amount, top, bound, skew):
    sequence = jax.random.permutation(key, amount)
    crowded, common = portions_of(amount, rows * top, bound, skew, True), portions_of(amount, rows * top, bound, skew, False)
    places = jnp.arange(amount)

    def named(sizes, offset_by):
        used = int((sizes > 0).sum())
        fixed = max(1, used // 4)
        shifted = fixed + (places - fixed + offset_by * (used - fixed)) % max(1, amount - fixed)
        return jnp.zeros((amount,), jnp.int32).at[sequence[jnp.where(places < fixed, places, shifted)]].set(jnp.asarray(sizes, jnp.int32))

    sizes = jnp.where(number % 4 == 0, named(crowded, number // 4), named(common, number - number // 4 - 1))
    mixed = jax.random.permutation(jax.random.fold_in(own, 3), amount)
    source_of, sink = mixed[0:amount // 2 * 2:2], mixed[1:amount // 2 * 2:2]
    slack = jnp.minimum(sizes[source_of] - 1, bound - sizes[sink]) // 2
    slack = jnp.where((source_of == sequence[0]) | (sink == sequence[0]) | (sizes[sink] == 0), 0, jnp.maximum(slack, 0))
    shifted = jax.random.randint(jax.random.fold_in(own, 4), (amount // 2,), 0, 1 << 20) % (slack + 1)
    sizes = sizes.at[source_of].add(-shifted).at[sink].add(shifted)
    labels = jnp.searchsorted(jnp.cumsum(sizes), jnp.arange(rows * top), side="right").astype(jnp.int32)
    listing = labels.reshape(top, rows).T
    listing = listing[jax.random.permutation(jax.random.fold_in(own, 1), rows)]
    offset_by = jax.random.randint(jax.random.fold_in(own, 2), (rows, 1), 0, top)
    return jnp.take_along_axis(listing, (jnp.arange(top)[None, :] + offset_by) % top, axis=1)


def portions_of(count, total, limit, lean, full):
    loads = [(1 << 20) // math.isqrt(grade ** lean) + 1 for grade in range(1, count + 1)]
    largest = limit if full else min(limit, max(-(-total // count), total * loads[0] // sum(loads)))
    least = 1 if total - largest >= count - 1 else 0
    given, rest = [largest] + [least] * (count - 1), total - largest - least * (count - 1)
    while rest > 0:
        free = [i for i in range(1, count) if given[i] < largest] or [i for i in range(1, count) if given[i] < limit]
        mass, budget = sum([loads[i] for i in free]), rest
        for i in free:
            addition = min(limit - given[i], max(1, budget * loads[i] // mass), rest)
            given[i] = given[i] + addition
            rest = rest - addition
    return np.array(given)


def bell_draw(own_key, dims, width, limit, cuts=(), held_as=jnp.bfloat16):
    entries = jax.random.normal(own_key, dims, jnp.float32) * width
    if len(cuts) > 0:
        entries = level_of(own_key, dims, cuts, -0.22, 0.18) * entries
    return jnp.clip(entries, min=-limit, max=limit).astype(held_as)


def bell_draw_with(own_key, shape, width, limit, cuts, heavy, held_as=jnp.bfloat16):
    values = width * jax.random.normal(own_key, shape, jnp.float32)
    if cuts:
        values = values * level_of(own_key, shape, cuts, -0.22, 0.18)
    return jnp.clip(spiked(values, jax.random.fold_in(own_key, 3), *heavy), -limit, limit).astype(held_as)


def setup_inputs(seed: int = 0) -> dict:
    streams_of = jax.random.split(jax.random.key(seed), 7)
    tokens = bell_draw(streams_of[0], (TOKENS, D), 1.0, 6.0, ((0, 16), (1, 32)))
    routes_keys = jax.random.split(jax.random.fold_in(streams_of[1], 1), TOKENS // TOK_DEV)
    routes_turns = jax.random.permutation(jax.random.fold_in(streams_of[1], 3), TOKENS // TOK_DEV)
    routes = jax.vmap(lambda own, number: routed_block(jax.random.fold_in(streams_of[1], 2), own, number, TOK_DEV, EXPERTS, 2, CAP, 2))(routes_keys, routes_turns).reshape((TOKENS, 2))
    route_weight = jnp.clip(0.25 + 0.75 * jax.random.uniform(streams_of[2], (TOKENS, 2), jnp.float32) ** level_of(streams_of[2], (TOKENS, 2), ((0, 16),), -0.2, 0.2), 0.25, 1.0)
    gate_weight = bell_draw(streams_of[3], (N_EXPERT, FF // 2, D), D ** -0.5, 0.09375, ((0, 16), (1, 32)))
    up_weight = bell_draw(streams_of[4], (N_EXPERT, FF // 2, D), D ** -0.5, 0.09375, ((0, 16), (1, 32)))
    down_weight = bell_draw_with(streams_of[5], (N_EXPERT, FF // 2, D), FF ** -0.5, 0.109375, ((0, 16), (1, 32)), (1, 2, 32, 2.75))
    return {"tokens": tokens, "routes": routes, "route_weight": route_weight, "gate_weight": gate_weight, "up_weight": up_weight, "down_weight": down_weight}


def slot_positions(route_block, experts, capacity):
    flat_routes = route_block.reshape(-1)
    onehot = (flat_routes[:, None] == jnp.arange(experts, dtype=jnp.int32)[None, :]).astype(jnp.int32)
    earlier = jnp.cumsum(onehot, axis=0) - onehot
    slot_index = jnp.sum(earlier * onehot, axis=1).astype(jnp.int32)
    return (flat_routes * capacity + slot_index).reshape(route_block.shape).astype(jnp.int32)


def feature_product(rows, weight_rows):
    return lax.dot_general(rows, weight_rows, (((1,), (1,)), ((), ())), preferred_element_type=jnp.float32)


def reference(tokens, routes, route_weight, gate_weight, up_weight, down_weight):
    groups = N_EXPERT
    blocks = routes.reshape(groups, TOK_DEV, 2)
    positions = jax.vmap(lambda route_block: slot_positions(route_block, EXPERTS, CAP))(blocks)
    slot_index = positions - blocks * CAP
    source = jnp.arange(groups, dtype=jnp.int32)[:, None, None]
    buffer_row = (source * CAP + slot_index).astype(jnp.int32)
    token_blocks = tokens.reshape(groups, TOK_DEV, D)
    repeated = jnp.broadcast_to(token_blocks[:, :, None, :], (groups, TOK_DEV, 2, D))
    buffers = jnp.zeros((EXPERTS, groups * CAP, D), tokens.dtype)
    buffers = buffers.at[blocks.reshape(-1), buffer_row.reshape(-1)].set(repeated.reshape(-1, D))
    half_width = FF // 2
    shard_width = half_width // N_TENSOR
    gate_pairs = gate_weight.reshape(EXPERTS, 2, half_width, D)
    up_pairs = up_weight.reshape(EXPERTS, 2, half_width, D)
    down_pairs = down_weight.reshape(EXPERTS, 2, half_width, D)

    def one_expert(operands):
        buffer, w_gate, w_up, w_down = operands
        halves = []
        for half in range(2):
            gate_sum = feature_product(buffer, w_gate[half])
            up_sum = feature_product(buffer, w_up[half])
            hidden = (jax.nn.silu(gate_sum) * up_sum).astype(jnp.bfloat16)
            hidden_shares = hidden.reshape(hidden.shape[0], N_TENSOR, shard_width).transpose(1, 0, 2)
            down_shares = w_down[half].reshape(N_TENSOR, shard_width, D)

            def add_share(totals, pair):
                share_rows, share_down = pair
                term = jnp.dot(share_rows, share_down, preferred_element_type=jnp.float32).astype(jnp.bfloat16)
                return totals + term.astype(jnp.float32), None

            start_sum = jnp.zeros((hidden.shape[0], D), jnp.float32)
            totals, _ = lax.scan(add_share, start_sum, (hidden_shares, down_shares))
            halves.append(totals.astype(jnp.bfloat16))
        return jnp.stack(halves)

    half_rows = lax.map(one_expert, (buffers, gate_pairs, up_pairs, down_pairs))
    picked = half_rows[blocks, :, buffer_row]
    picked = lax.optimization_barrier(picked).astype(jnp.float32)
    joined = jnp.sum(picked, axis=3)
    weights = route_weight.reshape(groups, TOK_DEV, 2)
    mixed = jnp.sum(weights[..., None] * joined, axis=2)
    return mixed.reshape(TOKENS, D).astype(jnp.bfloat16)
```

```python
import jax
import jax.numpy as jnp
from jax import lax
from jax.experimental import pallas as pl
from jax.experimental.pallas import tpu as pltpu
from jax.sharding import Mesh
from jax.sharding import PartitionSpec as P

BF = jnp.bfloat16
F32 = jnp.float32
TENSOR = ("tensor_0", "tensor_1")


def split_weights(core, gate, up, down):
    units, width = gate.shape
    half = width // 2
    step = 512

    def kernel(core_ref, g_ref, u_ref, d_ref, kg_ref, ku_ref, kd_ref, send_ref):
        c = core_ref[0]
        for i, (src, keep) in enumerate(((g_ref, kg_ref), (u_ref, ku_ref), (d_ref, kd_ref))):
            for j in range(step // 128):
                mine = pl.multiple_of((2 * j + c) * 128, 128)
                other = pl.multiple_of((2 * j + 1 - c) * 128, 128)
                keep[:, j * 128 : (j + 1) * 128] = src[:, pl.ds(mine, 128)]
                send_ref[i, :, j * 128 : (j + 1) * 128] = src[:, pl.ds(other, 128)]

    src_spec = pl.BlockSpec((units, 2 * step), lambda i, c: (0, i))
    keep_spec = pl.BlockSpec((units, step), lambda i, c: (0, i))
    return pl.pallas_call(
        kernel,
        grid_spec=pltpu.PrefetchScalarGridSpec(
            num_scalar_prefetch=1,
            grid=(half // step,),
            in_specs=[src_spec] * 3,
            out_specs=[keep_spec] * 3 + [pl.BlockSpec((3, units, step), lambda i, c: (0, 0, i))],
        ),
        out_shape=[jax.ShapeDtypeStruct((units, half), BF)] * 3
        + [jax.ShapeDtypeStruct((3, units, half), BF)],
        name="split_weights",
        cost_estimate=pl.CostEstimate(flops=0, bytes_accessed=12 * units * width, transcendentals=0),
    )(core, gate, up, down)


def dispatch(select, gathered, experts, capacity):
    planes, rows, lanes = gathered.shape
    per = 4

    def kernel(s_ref, x_ref, o_ref):
        x = jnp.concatenate([x_ref[k] for k in range(per)], axis=1)
        y = jnp.dot(s_ref[...], x, preferred_element_type=F32).astype(BF)
        y = y.reshape(experts, capacity, per * lanes)
        o_ref[:, 0] = y
        o_ref[:, 1] = y

    return pl.pallas_call(
        kernel,
        grid=(planes // per,),
        in_specs=[
            pl.BlockSpec(select.shape, lambda i: (0, 0)),
            pl.BlockSpec((per, rows, lanes), lambda i: (i, 0, 0)),
        ],
        out_specs=pl.BlockSpec((experts, 2, capacity, per * lanes), lambda i: (0, 0, 0, i)),
        out_shape=jax.ShapeDtypeStruct((experts, 2, capacity, planes * lanes), BF),
        name="dispatch",
    )(select, gathered)


def padded(units):
    return -(-units // 8) * 8


def dot_last(a, b):
    return lax.dot_general(a, b, (((1,), (1,)), ((), ())), preferred_element_type=F32)


def gate_up(rows_in, keep_gate, keep_up, other):
    count, half = rows_in.shape
    units = keep_gate.shape[0]
    tall = padded(units)
    step = 512

    def kernel(x_ref, g_ref, u_ref, og_ref, ou_ref, o_ref):
        x = x_ref[...]
        parts = (g_ref[...], og_ref[0], u_ref[...], ou_ref[0])
        first = pl.program_id(0) == 0
        for i, w in enumerate(parts):
            total = dot_last(w, x)

            @pl.when(first)
            def _():
                o_ref[i * tall : i * tall + units] = total

            @pl.when(jnp.logical_not(first))
            def _():
                o_ref[i * tall : i * tall + units] += total

    return pl.pallas_call(
        kernel,
        grid=(half // step,),
        in_specs=[
            pl.BlockSpec((count, step), lambda i: (0, i)),
            pl.BlockSpec((units, step), lambda i: (0, i)),
            pl.BlockSpec((units, step), lambda i: (0, i)),
            pl.BlockSpec((1, units, step), lambda i: (0, 0, i)),
            pl.BlockSpec((1, units, step), lambda i: (1, 0, i)),
        ],
        out_specs=pl.BlockSpec((4 * tall, count), lambda i: (0, 0)),
        out_shape=jax.ShapeDtypeStruct((4 * tall, count), F32),
        name="gate_up",
    )(rows_in, keep_gate, keep_up, other, other)


def down_rows(own, received, keep_down, other):
    count = own.shape[1]
    units, half = keep_down.shape
    tall = padded(units)
    step = 512

    def part(ref, k):
        return ref[k * tall : k * tall + units]

    def kernel(p_ref, r_ref, d_ref, od_ref, o_ref, mine, partner):
        @pl.when(pl.program_id(0) == 0)
        def _():
            for k, out in ((0, mine), (1, partner)):
                gate = part(p_ref, k) + part(r_ref, 1 - k)
                up = part(p_ref, 2 + k) + part(r_ref, 3 - k)
                hidden = gate / (1.0 + jnp.exp(-gate)) * up
                out[...] = hidden.T.astype(BF)

        total = jnp.dot(mine[...], d_ref[...], preferred_element_type=F32)
        total += jnp.dot(partner[...], od_ref[0], preferred_element_type=F32)
        o_ref[...] = total.astype(BF)

    whole = pl.BlockSpec((4 * tall, count), lambda i: (0, 0))
    return pl.pallas_call(
        kernel,
        grid=(half // step,),
        in_specs=[
            whole,
            whole,
            pl.BlockSpec((units, step), lambda i: (0, i)),
            pl.BlockSpec((1, units, step), lambda i: (2, 0, i)),
        ],
        out_specs=pl.BlockSpec((count, step), lambda i: (0, i)),
        out_shape=jax.ShapeDtypeStruct((count, half), BF),
        scratch_shapes=[pltpu.VMEM((count, units), BF)] * 2,
        name="down_rows",
    )(own, received, keep_down, other)


def combine(weights, returned, planes):
    twice, slots = weights.shape
    rows = twice // 2
    half = returned.shape[1]
    lanes = half // planes
    per = 4

    def kernel(w_ref, r_ref, o_ref):
        total = jnp.dot(w_ref[...], r_ref[...], preferred_element_type=F32)
        total = (total[:rows] + total[rows:]).astype(BF)
        for k in range(per):
            o_ref[k] = total[:, k * lanes : (k + 1) * lanes]

    return pl.pallas_call(
        kernel,
        grid=(planes // per,),
        in_specs=[
            pl.BlockSpec((twice, slots), lambda i: (0, 0)),
            pl.BlockSpec((slots, per * lanes), lambda i: (0, i)),
        ],
        out_specs=pl.BlockSpec((per, rows, lanes), lambda i: (i, 0, 0)),
        out_shape=jax.ShapeDtypeStruct((planes, rows, lanes), BF),
        name="combine",
    )(weights, returned)


def slot_positions(route_block, experts, capacity):
    flat_routes = route_block.reshape(-1)
    onehot = (flat_routes[:, None] == jnp.arange(experts, dtype=jnp.int32)[None, :]).astype(
        jnp.int32
    )
    earlier = jnp.cumsum(onehot, axis=0) - onehot
    slot_index = jnp.sum(earlier * onehot, axis=1)
    return (flat_routes * capacity + slot_index).reshape(route_block.shape)


def local(tokens, routes, route_weight, gate_weight, up_weight, down_weight):
    group_count = lax.axis_size("expert")
    planes = lax.axis_size("tensor_0")
    experts = group_count // 2
    tok_rows, lanes = tokens.shape
    capacity = min(tok_rows, 4 * tok_rows // experts)
    slots_out = experts * capacity
    slots_in = group_count * capacity
    half = planes * lanes
    core = lax.axis_index("tensor_1").astype(jnp.int32).reshape(1)

    spread = jnp.broadcast_to(tokens[None], (planes, tok_rows, lanes))
    gathered = lax.all_to_all(spread, "tensor_0", split_axis=0, concat_axis=0, tiled=True)

    positions = slot_positions(routes, experts, capacity)
    slot_ids = jnp.arange(slots_out, dtype=jnp.int32)
    matches = positions[:, :, None] == slot_ids[None, None, :]
    select = jnp.any(matches, axis=1).astype(BF).T
    mix = jnp.sum(jnp.where(matches, route_weight[:, :, None], 0.0), axis=1)
    mix = mix.reshape(tok_rows, experts, 1, capacity)
    mix = jnp.broadcast_to(mix, (tok_rows, experts, 2, capacity)).reshape(tok_rows, slots_in)
    high = lax.reduce_precision(mix, 8, 7)
    mix = jnp.concatenate([high, mix - high], axis=0).astype(BF)

    keep_gate, keep_up, keep_down, send = split_weights(
        core, gate_weight[0], up_weight[0], down_weight[0]
    )
    swap = [(0, 1), (1, 0)]
    other = lax.ppermute(send, "tensor_1", swap)

    outgoing = dispatch(select, gathered, experts, capacity)
    outgoing = outgoing.reshape(group_count, capacity, half)
    incoming = lax.all_to_all(outgoing, "expert", split_axis=0, concat_axis=0, tiled=True)
    incoming = incoming.reshape(slots_in, half)

    own = gate_up(incoming, keep_gate, keep_up, other)
    received = lax.ppermute(own, "tensor_1", swap)
    result = down_rows(own, received, keep_down, other)

    result = result.reshape(group_count, capacity, half)
    returned = lax.all_to_all(result, "expert", split_axis=0, concat_axis=0, tiled=True)
    blocks = combine(mix, returned.reshape(slots_in, half), planes)
    blocks = lax.all_to_all(blocks, "tensor_0", split_axis=0, concat_axis=0, tiled=True)
    return jnp.sum(blocks.astype(F32), axis=0).astype(BF)


def solution(mesh):
    torus = Mesh(
        mesh.devices.reshape(mesh.shape["expert"], 16, 2), ("expert", "tensor_0", "tensor_1")
    )
    placed = (
        P("expert", TENSOR),
        P("expert", None),
        P("expert", None),
        P("expert", TENSOR, None),
        P("expert", TENSOR, None),
        P("expert", TENSOR, None),
    )
    return jax.shard_map(
        local, mesh=torus, in_specs=placed, out_specs=P("expert", TENSOR), check_vma=False
    )
```

```python
import jax
import jax.numpy as jnp
from jax import lax
from jax.experimental import pallas as pl
from jax.experimental.pallas import tpu as pltpu
from jax.sharding import Mesh
from jax.sharding import PartitionSpec as P

BF = jnp.bfloat16
F32 = jnp.float32
TENSOR = ("far", "near", "core")
WIDE = ("expert", "near", "core")
ANY = pl.BlockSpec(memory_space=pl.ANY)
VMEM = pl.BlockSpec(memory_space=pltpu.VMEM)


def params(mib):
    return pltpu.CompilerParams(vmem_limit_bytes=mib * 2**20)


def dispatch(select, gathered, experts, cores):
    planes, rows, lanes = gathered.shape
    slots = select.shape[0] // experts // cores
    width = planes * lanes
    per = 4
    steps = planes // per

    def kernel(s_ref, x_ref, o_ref, held, sem):
        s = s_ref[...]
        copies = []
        for k in range(steps):
            x = jnp.concatenate([x_ref[per * k + i] for i in range(per)], axis=1)
            y = jnp.dot(s, x, preferred_element_type=F32).astype(BF)
            held[k] = y.reshape(experts, cores, slots, per * lanes)
            for i in range(4):
                at = pl.ds(k * per * lanes, per * lanes)
                out = o_ref.at[:, i // 2, i % 2, :, :, at]
                copies.append(pltpu.make_async_copy(held.at[k], out, sem.at[k, i]))
                copies[-1].start()
        for copy in copies:
            copy.wait()

    return pl.pallas_call(
        kernel,
        in_specs=[VMEM] * 2,
        out_specs=ANY,
        out_shape=jax.ShapeDtypeStruct((experts, 2, 2, cores, slots, width), BF),
        scratch_shapes=[
            pltpu.VMEM((steps, experts, cores, slots, per * lanes), BF),
            pltpu.SemaphoreType.DMA((steps, 4)),
        ],
        compiler_params=params(8),
        name="dispatch",
    )(select, gathered)


def feed_forward(incoming, own, other):
    blocks, slots, width = incoming.shape
    units, features = own[0].shape
    ways = features // width
    groups = blocks // ways
    rows = groups * slots
    tall = -(-units // 16) * 16
    steps = 4
    lanes = width // steps
    span = lanes * ways
    parts = lanes // 128

    def stack(ref, step, count):
        blank = jnp.zeros((tall - units, span), BF)
        pieces = [piece for i in range(count) for piece in (ref[step, i], blank)]
        return jnp.concatenate(pieces, axis=0)

    def kernel(x_ref, g, u, d, og, ou, od, o_ref, xs, ws, ds, total, hidden, ys, sx, sw, sd, so):
        first, last = (g, og, u, ou), (d, od)
        loads = []
        for t in range(steps):
            at = pl.ds(t * span, span)
            load = [
                pltpu.make_async_copy(x_ref.at[:, :, pl.ds(t * lanes, lanes)], xs.at[t], sx.at[t])
            ]
            for i, w in enumerate(first):
                load.append(pltpu.make_async_copy(w.at[:, at], ws.at[t, i], sw.at[t, i]))
            loads.append(load)
        for t in range(steps):
            at = pl.ds(t * span, span)
            loads.append(
                [
                    pltpu.make_async_copy(w.at[:, at], ds.at[t, i], sd.at[t, i])
                    for i, w in enumerate(last)
                ]
            )
        for load in loads:
            for copy in load:
                copy.start()

        for t in range(steps):
            for copy in loads[t]:
                copy.wait()
            x = xs[t].reshape(groups, ways, slots, lanes)
            x = jnp.concatenate(
                [
                    x[:, k, :, p * 128 : (p + 1) * 128].reshape(rows, 128)
                    for p in range(parts)
                    for k in range(ways)
                ],
                axis=1,
            )
            part = lax.dot_general(
                x, stack(ws, t, 4), (((1,), (1,)), ((), ())), preferred_element_type=F32
            )
            if t == 0:
                total[...] = part
            else:
                total[...] += part
        gate, up = total[:, : 2 * tall], total[:, 2 * tall :]
        hidden[...] = (gate / (1.0 + jnp.exp(-gate)) * up).astype(BF)

        stores = []
        for t in range(steps):
            for copy in loads[steps + t]:
                copy.wait()
            y = jnp.dot(hidden[...], stack(ds, t, 2), preferred_element_type=F32).astype(BF)
            for p in range(parts):
                for k in range(ways):
                    at = (p * ways + k) * 128
                    ys[t, :, k, :, p * 128 : (p + 1) * 128] = y[:, at : at + 128].reshape(
                        groups, slots, 128
                    )
            out = o_ref.at[:, :, :, pl.ds(t * lanes, lanes)]
            stores.append(pltpu.make_async_copy(ys.at[t], out, so.at[t]))
            stores[-1].start()
        for copy in stores:
            copy.wait()

    out = pl.pallas_call(
        kernel,
        in_specs=[ANY] * 7,
        out_specs=ANY,
        out_shape=jax.ShapeDtypeStruct((groups, ways, slots, width), BF),
        scratch_shapes=[
            pltpu.VMEM((steps, blocks, slots, lanes), BF),
            pltpu.VMEM((steps, 4, units, span), BF),
            pltpu.VMEM((steps, 2, units, span), BF),
            pltpu.VMEM((rows, 4 * tall), F32),
            pltpu.VMEM((rows, 2 * tall), BF),
            pltpu.VMEM((steps, groups, ways, slots, lanes), BF),
            pltpu.SemaphoreType.DMA((steps,)),
            pltpu.SemaphoreType.DMA((steps, 4)),
            pltpu.SemaphoreType.DMA((steps, 2)),
            pltpu.SemaphoreType.DMA((steps,)),
        ],
        compiler_params=params(48),
        name="feed_forward",
    )(incoming, *own, *other)
    return out.reshape(blocks, slots, width)


def combine(weights, returned, planes):
    twice = weights.shape[0]
    rows = twice // 2
    lanes = returned.shape[1] // planes

    def kernel(w_ref, r_ref, o_ref):
        w = w_ref[...]
        for k in range(0, planes, 2):
            total = jnp.dot(w, r_ref[:, k * lanes : (k + 2) * lanes], preferred_element_type=F32)
            total = (total[:rows] + total[rows:]).astype(BF)
            o_ref[k] = total[:, :lanes]
            o_ref[k + 1] = total[:, lanes:]

    return pl.pallas_call(
        kernel,
        in_specs=[VMEM] * 2,
        out_specs=VMEM,
        out_shape=jax.ShapeDtypeStruct((planes, rows, lanes), BF),
        compiler_params=params(8),
        name="combine",
    )(weights, returned)


def slot_positions(route_block, experts, capacity):
    flat_routes = route_block.reshape(-1)
    onehot = (flat_routes[:, None] == jnp.arange(experts, dtype=jnp.int32)[None, :]).astype(
        jnp.int32
    )
    earlier = jnp.cumsum(onehot, axis=0) - onehot
    slot_index = jnp.sum(earlier * onehot, axis=1)
    return (flat_routes * capacity + slot_index).reshape(route_block.shape)


def exchange(blocks, axes):
    return lax.all_to_all(blocks, axes, split_axis=0, concat_axis=0, tiled=True)


def local(tokens, routes, route_weight, gate_weight, up_weight, down_weight):
    group_count = lax.axis_size("expert")
    planes = lax.axis_size("far")
    cores = lax.axis_size("core")
    experts = group_count // 2
    tok_rows, lanes = tokens.shape
    capacity = min(tok_rows, 4 * tok_rows // experts)
    slots_out = experts * capacity
    slots = capacity // cores
    blocks = group_count * 2 * cores
    width = planes * lanes

    gathered = exchange(jnp.broadcast_to(tokens[None], (planes, tok_rows, lanes)), "far")

    positions = slot_positions(routes, experts, capacity)
    slot_ids = jnp.arange(slots_out, dtype=jnp.int32)
    matches = positions[:, :, None] == slot_ids[None, None, :]
    select = jnp.any(matches, axis=1).astype(BF).T
    mix = jnp.sum(jnp.where(matches, route_weight[:, :, None], 0.0), axis=1)
    mix = mix.reshape(tok_rows, experts, 1, capacity)
    mix = jnp.broadcast_to(mix, (tok_rows, experts, 4, capacity)).reshape(tok_rows, 4 * slots_out)
    high = lax.reduce_precision(mix, 8, 7)
    mix = jnp.concatenate([high, mix - high], axis=0).astype(BF)

    outgoing = dispatch(select, gathered, experts, cores)
    own = (gate_weight[0], up_weight[0], down_weight[0])
    other = tuple(lax.ppermute(w, "core", [(0, 1), (1, 0)]) for w in own)
    incoming = exchange(outgoing.reshape(blocks, slots, width), WIDE)

    result = feed_forward(incoming, own, other)

    returned = exchange(result, WIDE)
    mixed = combine(mix, returned.reshape(blocks * slots, width), planes)
    mixed = exchange(mixed, "far")
    return jnp.sum(mixed.astype(F32), axis=0).astype(BF)


def solution(mesh):
    torus = Mesh(
        mesh.devices.reshape(mesh.shape["expert"], 8, 2, 2), ("expert", "far", "near", "core")
    )
    placed = (
        P("expert", TENSOR),
        P("expert", None),
        P("expert", None),
        P("expert", TENSOR, None),
        P("expert", TENSOR, None),
        P("expert", TENSOR, None),
    )
    return jax.shard_map(
        local, mesh=torus, in_specs=placed, out_specs=P("expert", TENSOR), check_vma=False
    )
```

```python
import jax
import jax.numpy as jnp
from jax import lax
from jax.experimental import pallas as pl
from jax.experimental.pallas import tpu as pltpu
from jax.sharding import Mesh
from jax.sharding import PartitionSpec as P

BF = jnp.bfloat16
F32 = jnp.float32
TENSOR = ("far", "near", "core")
WIDE = ("expert", "near", "core")
ANY = pl.BlockSpec(memory_space=pl.ANY)
VMEM = pl.BlockSpec(memory_space=pltpu.VMEM)


def params(mib):
    return pltpu.CompilerParams(vmem_limit_bytes=mib * 2**20)


def dispatch(select, gathered, experts, cores):
    planes, rows, lanes = gathered.shape
    slots = select.shape[0] // experts // cores
    width = planes * lanes
    per = 4
    steps = planes // per

    def kernel(s_ref, x_ref, o_ref, held, sem):
        s = s_ref[...]
        copies = []
        for k in range(steps):
            x = jnp.concatenate([x_ref[per * k + i] for i in range(per)], axis=1)
            y = jnp.dot(s, x, preferred_element_type=F32).astype(BF)
            held[k] = y.reshape(experts, cores, slots, per * lanes)
            for i in range(4):
                at = pl.ds(k * per * lanes, per * lanes)
                out = o_ref.at[:, i // 2, i % 2, :, :, at]
                copies.append(pltpu.make_async_copy(held.at[k], out, sem.at[k, i]))
                copies[-1].start()
        for copy in copies:
            copy.wait()

    return pl.pallas_call(
        kernel,
        in_specs=[VMEM] * 2,
        out_specs=ANY,
        out_shape=jax.ShapeDtypeStruct((experts, 2, 2, cores, slots, width), BF),
        scratch_shapes=[
            pltpu.VMEM((steps, experts, cores, slots, per * lanes), BF),
            pltpu.SemaphoreType.DMA((steps, 4)),
        ],
        compiler_params=params(8),
        name="dispatch",
    )(select, gathered)


def stack_weights(own, other):
    units, features = own[0].shape
    tall = -(-units // 16) * 16
    span = features // 4

    def kernel(g, u, d, og, ou, od, first_ref, last_ref):
        blank = jnp.zeros((tall - units, span), BF)
        for i, src in enumerate((g, og, u, ou)):
            first_ref[i * tall : (i + 1) * tall] = jnp.concatenate([src[...], blank], axis=0)
        for i, src in enumerate((d, od)):
            last_ref[i * tall : (i + 1) * tall] = jnp.concatenate([src[...], blank], axis=0)

    def columns(rows):
        return pl.BlockSpec((rows, span), lambda i: (0, i))

    return pl.pallas_call(
        kernel,
        grid=(4,),
        in_specs=[columns(units)] * 6,
        out_specs=[columns(4 * tall), columns(2 * tall)],
        out_shape=[
            jax.ShapeDtypeStruct((4 * tall, features), BF),
            jax.ShapeDtypeStruct((2 * tall, features), BF),
        ],
        compiler_params=params(63),
        name="stack_weights",
        cost_estimate=pl.CostEstimate(
            flops=0, bytes_accessed=24 * units * features, transcendentals=0
        ),
    )(*own, *other)


def feed_forward(incoming, first, last):
    blocks, slots, width = incoming.shape
    tall, features = last.shape
    ways = features // width
    groups = blocks // ways
    rows = groups * slots
    steps = 4
    lanes = width // steps
    span = lanes * ways
    parts = lanes // 128

    def kernel(x_ref, f_ref, l_ref, o_ref, xs, ws, ds, total, hidden, ys, sx, sw, sd, so):
        loads = []
        for t in range(steps):
            at = pl.ds(t * span, span)
            x_at = x_ref.at[:, :, pl.ds(t * lanes, lanes)]
            loads.append(
                [
                    pltpu.make_async_copy(x_at, xs.at[t], sx.at[t]),
                    pltpu.make_async_copy(f_ref.at[:, at], ws.at[t], sw.at[t]),
                ]
            )
        for t in range(steps):
            at = pl.ds(t * span, span)
            loads.append([pltpu.make_async_copy(l_ref.at[:, at], ds.at[t], sd.at[t])])
        for load in loads:
            for copy in load:
                copy.start()

        for t in range(steps):
            for copy in loads[t]:
                copy.wait()
            x = xs[t].reshape(groups, ways, slots, lanes)
            x = jnp.concatenate(
                [
                    x[:, k, :, p * 128 : (p + 1) * 128].reshape(rows, 128)
                    for p in range(parts)
                    for k in range(ways)
                ],
                axis=1,
            )
            part = lax.dot_general(
                x, ws[t], (((1,), (1,)), ((), ())), preferred_element_type=F32
            )
            if t == 0:
                total[...] = part
            else:
                total[...] += part
        gate, up = total[:, :tall], total[:, tall:]
        hidden[...] = (gate / (1.0 + jnp.exp(-gate)) * up).astype(BF)

        stores = []
        for t in range(steps):
            for copy in loads[steps + t]:
                copy.wait()
            y = jnp.dot(hidden[...], ds[t], preferred_element_type=F32).astype(BF)
            for p in range(parts):
                for k in range(ways):
                    at = (p * ways + k) * 128
                    ys[t, :, k, :, p * 128 : (p + 1) * 128] = y[:, at : at + 128].reshape(
                        groups, slots, 128
                    )
            out = o_ref.at[:, :, :, pl.ds(t * lanes, lanes)]
            stores.append(pltpu.make_async_copy(ys.at[t], out, so.at[t]))
            stores[-1].start()
        for copy in stores:
            copy.wait()

    out = pl.pallas_call(
        kernel,
        in_specs=[ANY] * 3,
        out_specs=ANY,
        out_shape=jax.ShapeDtypeStruct((groups, ways, slots, width), BF),
        scratch_shapes=[
            pltpu.VMEM((steps, blocks, slots, lanes), BF),
            pltpu.VMEM((steps, 2 * tall, span), BF),
            pltpu.VMEM((steps, tall, span), BF),
            pltpu.VMEM((rows, 2 * tall), F32),
            pltpu.VMEM((rows, tall), BF),
            pltpu.VMEM((steps, groups, ways, slots, lanes), BF),
            pltpu.SemaphoreType.DMA((steps,)),
            pltpu.SemaphoreType.DMA((steps,)),
            pltpu.SemaphoreType.DMA((steps,)),
            pltpu.SemaphoreType.DMA((steps,)),
        ],
        compiler_params=params(63),
        name="feed_forward",
    )(incoming, first, last)
    return out.reshape(blocks, slots, width)


def combine(weights, returned, planes):
    twice = weights.shape[0]
    rows = twice // 2
    lanes = returned.shape[1] // planes

    def kernel(w_ref, r_ref, o_ref):
        w = w_ref[...]
        for k in range(0, planes, 2):
            total = jnp.dot(w, r_ref[:, k * lanes : (k + 2) * lanes], preferred_element_type=F32)
            total = (total[:rows] + total[rows:]).astype(BF)
            o_ref[k] = total[:, :lanes]
            o_ref[k + 1] = total[:, lanes:]

    return pl.pallas_call(
        kernel,
        in_specs=[VMEM] * 2,
        out_specs=VMEM,
        out_shape=jax.ShapeDtypeStruct((planes, rows, lanes), BF),
        compiler_params=params(8),
        name="combine",
    )(weights, returned)


def slot_positions(route_block, experts, capacity):
    flat_routes = route_block.reshape(-1)
    onehot = (flat_routes[:, None] == jnp.arange(experts, dtype=jnp.int32)[None, :]).astype(
        jnp.int32
    )
    earlier = jnp.cumsum(onehot, axis=0) - onehot
    slot_index = jnp.sum(earlier * onehot, axis=1)
    return (flat_routes * capacity + slot_index).reshape(route_block.shape)


def exchange(blocks, axes):
    return lax.all_to_all(blocks, axes, split_axis=0, concat_axis=0, tiled=True)


def local(tokens, routes, route_weight, gate_weight, up_weight, down_weight):
    group_count = lax.axis_size("expert")
    planes = lax.axis_size("far")
    cores = lax.axis_size("core")
    experts = group_count // 2
    tok_rows, lanes = tokens.shape
    capacity = min(tok_rows, 4 * tok_rows // experts)
    slots_out = experts * capacity
    slots = capacity // cores
    blocks = group_count * 2 * cores
    width = planes * lanes

    gathered = exchange(jnp.broadcast_to(tokens[None], (planes, tok_rows, lanes)), "far")

    positions = slot_positions(routes, experts, capacity)
    slot_ids = jnp.arange(slots_out, dtype=jnp.int32)
    matches = positions[:, :, None] == slot_ids[None, None, :]
    select = jnp.any(matches, axis=1).astype(BF).T
    mix = jnp.sum(jnp.where(matches, route_weight[:, :, None], 0.0), axis=1)
    mix = mix.reshape(tok_rows, experts, 1, capacity)
    mix = jnp.broadcast_to(mix, (tok_rows, experts, 4, capacity)).reshape(tok_rows, 4 * slots_out)
    high = lax.reduce_precision(mix, 8, 7)
    mix = jnp.concatenate([high, mix - high], axis=0).astype(BF)

    outgoing = dispatch(select, gathered, experts, cores)
    own = (gate_weight[0], up_weight[0], down_weight[0])
    other = tuple(lax.ppermute(w, "core", [(0, 1), (1, 0)]) for w in own)
    incoming = exchange(outgoing.reshape(blocks, slots, width), WIDE)
    first, last = stack_weights(own, other)

    result = feed_forward(incoming, first, last)

    returned = exchange(result, WIDE)
    mixed = combine(mix, returned.reshape(blocks * slots, width), planes)
    mixed = exchange(mixed, "far")
    return jnp.sum(mixed.astype(F32), axis=0).astype(BF)


def solution(mesh):
    torus = Mesh(
        mesh.devices.reshape(mesh.shape["expert"], 8, 2, 2), ("expert", "far", "near", "core")
    )
    placed = (
        P("expert", TENSOR),
        P("expert", None),
        P("expert", None),
        P("expert", TENSOR, None),
        P("expert", TENSOR, None),
        P("expert", TENSOR, None),
    )
    return jax.shard_map(
        local, mesh=torus, in_specs=placed, out_specs=P("expert", TENSOR), check_vma=False
    )
```

```python
import jax
import jax.numpy as jnp
from jax import lax
from jax.experimental import pallas as pl
from jax.experimental.pallas import tpu as pltpu
from jax.sharding import Mesh
from jax.sharding import PartitionSpec as P

BF = jnp.bfloat16
F32 = jnp.float32
TENSOR = ("far", "near", "core")
WIDE = ("expert", "near", "core")
ANY = pl.BlockSpec(memory_space=pl.ANY)
VMEM = pl.BlockSpec(memory_space=pltpu.VMEM)


def params(mib):
    return pltpu.CompilerParams(vmem_limit_bytes=mib * 2**20)


def dispatch(select, gathered, experts, cores):
    planes, rows, lanes = gathered.shape
    slots = select.shape[0] // experts // cores
    width = planes * lanes
    per = 4
    steps = planes // per

    def kernel(s_ref, x_ref, o_ref, held, sem):
        s = s_ref[...]
        copies = []
        for k in range(steps):
            x = jnp.concatenate([x_ref[per * k + i] for i in range(per)], axis=1)
            y = jnp.dot(s, x, preferred_element_type=F32).astype(BF)
            held[k] = y.reshape(experts, cores, slots, per * lanes)
            for i in range(4):
                at = pl.ds(k * per * lanes, per * lanes)
                out = o_ref.at[:, i // 2, i % 2, :, :, at]
                copies.append(pltpu.make_async_copy(held.at[k], out, sem.at[k, i]))
                copies[-1].start()
        for copy in copies:
            copy.wait()

    return pl.pallas_call(
        kernel,
        in_specs=[VMEM] * 2,
        out_specs=ANY,
        out_shape=jax.ShapeDtypeStruct((experts, 2, 2, cores, slots, width), BF),
        scratch_shapes=[
            pltpu.VMEM((steps, experts, cores, slots, per * lanes), BF),
            pltpu.SemaphoreType.DMA((steps, 4)),
        ],
        compiler_params=params(8),
        name="dispatch",
    )(select, gathered)


def stack_weights(own, other):
    units, features = own[0].shape
    tall = -(-units // 16) * 16
    span = features // 4

    def kernel(g, u, d, og, ou, od, first_ref, last_ref):
        blank = jnp.zeros((tall - units, span), BF)
        for i, src in enumerate((g, og, u, ou)):
            first_ref[i * tall : (i + 1) * tall] = jnp.concatenate([src[...], blank], axis=0)
        for i, src in enumerate((d, od)):
            last_ref[i * tall : (i + 1) * tall] = jnp.concatenate([src[...], blank], axis=0)

    def columns(rows):
        return pl.BlockSpec((rows, span), lambda i: (0, i))

    return pl.pallas_call(
        kernel,
        grid=(4,),
        in_specs=[columns(units)] * 6,
        out_specs=[columns(4 * tall), columns(2 * tall)],
        out_shape=[
            jax.ShapeDtypeStruct((4 * tall, features), BF),
            jax.ShapeDtypeStruct((2 * tall, features), BF),
        ],
        compiler_params=params(63),
        name="stack_weights",
        cost_estimate=pl.CostEstimate(
            flops=0, bytes_accessed=24 * units * features, transcendentals=0
        ),
    )(*own, *other)


def feed_forward(incoming, first, last):
    blocks, slots, width = incoming.shape
    tall, features = last.shape
    ways = features // width
    groups = blocks // ways
    rows = groups * slots
    steps = 4
    lanes = width // steps
    span = lanes * ways
    parts = lanes // 128
    halves = 2

    def kernel(x_ref, f_ref, l_ref, o_ref, xs, ws, ds, total, hidden, ys, sx, sw, sd, so):
        loads = []
        for t in range(steps):
            at = pl.ds(t * span, span)
            x_at = x_ref.at[:, :, pl.ds(t * lanes, lanes)]
            loads.append(
                [
                    pltpu.make_async_copy(x_at, xs.at[t], sx.at[t]),
                    pltpu.make_async_copy(f_ref.at[:, at], ws.at[t], sw.at[t]),
                ]
            )
        for t in range(halves):
            at = pl.ds(t * features // halves, features // halves)
            loads.append([pltpu.make_async_copy(l_ref.at[:, at], ds.at[t], sd.at[t])])
        for load in loads:
            for copy in load:
                copy.start()

        for t in range(steps):
            for copy in loads[t]:
                copy.wait()
            x = xs[t].reshape(groups, ways, slots, lanes)
            x = jnp.concatenate(
                [
                    x[:, k, :, p * 128 : (p + 1) * 128].reshape(rows, 128)
                    for p in range(parts)
                    for k in range(ways)
                ],
                axis=1,
            )
            part = lax.dot_general(
                x, ws[t], (((1,), (1,)), ((), ())), preferred_element_type=F32
            )
            if t == 0:
                total[...] = part
            else:
                total[...] += part
        gate, up = total[:, :tall], total[:, tall:]
        hidden[...] = (gate / (1.0 + jnp.exp(-gate)) * up).astype(BF)

        stores = []
        for t in range(halves):
            for copy in loads[steps + t]:
                copy.wait()
            y = jnp.dot(hidden[...], ds[t], preferred_element_type=F32).astype(BF)
            for p in range(width // halves // 128):
                for k in range(ways):
                    at = (p * ways + k) * 128
                    ys[t, :, k, :, p * 128 : (p + 1) * 128] = y[:, at : at + 128].reshape(
                        groups, slots, 128
                    )
            out = o_ref.at[:, :, :, pl.ds(t * width // halves, width // halves)]
            stores.append(pltpu.make_async_copy(ys.at[t], out, so.at[t]))
            stores[-1].start()
        for copy in stores:
            copy.wait()

    out = pl.pallas_call(
        kernel,
        in_specs=[ANY] * 3,
        out_specs=ANY,
        out_shape=jax.ShapeDtypeStruct((groups, ways, slots, width), BF),
        scratch_shapes=[
            pltpu.VMEM((steps, blocks, slots, lanes), BF),
            pltpu.VMEM((steps, 2 * tall, span), BF),
            pltpu.VMEM((halves, tall, features // halves), BF),
            pltpu.VMEM((rows, 2 * tall), F32),
            pltpu.VMEM((rows, tall), BF),
            pltpu.VMEM((halves, groups, ways, slots, width // halves), BF),
            pltpu.SemaphoreType.DMA((steps,)),
            pltpu.SemaphoreType.DMA((steps,)),
            pltpu.SemaphoreType.DMA((halves,)),
            pltpu.SemaphoreType.DMA((halves,)),
        ],
        compiler_params=params(63),
        name="feed_forward",
    )(incoming, first, last)
    return out.reshape(blocks, slots, width)


def combine(weights, returned, planes):
    twice = weights.shape[0]
    rows = twice // 2
    lanes = returned.shape[1] // planes

    def kernel(w_ref, r_ref, o_ref):
        w = w_ref[...]
        for k in range(0, planes, 2):
            total = jnp.dot(w, r_ref[:, k * lanes : (k + 2) * lanes], preferred_element_type=F32)
            total = (total[:rows] + total[rows:]).astype(BF)
            o_ref[k] = total[:, :lanes]
            o_ref[k + 1] = total[:, lanes:]

    return pl.pallas_call(
        kernel,
        in_specs=[VMEM] * 2,
        out_specs=VMEM,
        out_shape=jax.ShapeDtypeStruct((planes, rows, lanes), BF),
        compiler_params=params(8),
        name="combine",
    )(weights, returned)


def slot_positions(route_block, experts, capacity):
    flat_routes = route_block.reshape(-1)
    onehot = (flat_routes[:, None] == jnp.arange(experts, dtype=jnp.int32)[None, :]).astype(
        jnp.int32
    )
    earlier = jnp.cumsum(onehot, axis=0) - onehot
    slot_index = jnp.sum(earlier * onehot, axis=1)
    return (flat_routes * capacity + slot_index).reshape(route_block.shape)


def exchange(blocks, axes):
    return lax.all_to_all(blocks, axes, split_axis=0, concat_axis=0, tiled=True)


def local(tokens, routes, route_weight, gate_weight, up_weight, down_weight):
    group_count = lax.axis_size("expert")
    planes = lax.axis_size("far")
    cores = lax.axis_size("core")
    experts = group_count // 2
    tok_rows, lanes = tokens.shape
    capacity = min(tok_rows, 4 * tok_rows // experts)
    slots_out = experts * capacity
    slots = capacity // cores
    blocks = group_count * 2 * cores
    width = planes * lanes

    gathered = exchange(jnp.broadcast_to(tokens[None], (planes, tok_rows, lanes)), "far")

    positions = slot_positions(routes, experts, capacity)
    slot_ids = jnp.arange(slots_out, dtype=jnp.int32)
    matches = positions[:, :, None] == slot_ids[None, None, :]
    select = jnp.any(matches, axis=1).astype(BF).T
    mix = jnp.sum(jnp.where(matches, route_weight[:, :, None], 0.0), axis=1)
    mix = mix.reshape(tok_rows, experts, 1, capacity)
    mix = jnp.broadcast_to(mix, (tok_rows, experts, 4, capacity)).reshape(tok_rows, 4 * slots_out)
    high = lax.reduce_precision(mix, 8, 7)
    mix = jnp.concatenate([high, mix - high], axis=0).astype(BF)

    outgoing = dispatch(select, gathered, experts, cores)
    own = (gate_weight[0], up_weight[0], down_weight[0])
    other = tuple(lax.ppermute(w, "core", [(0, 1), (1, 0)]) for w in own)
    incoming = exchange(outgoing.reshape(blocks, slots, width), WIDE)
    first, last = stack_weights(own, other)

    result = feed_forward(incoming, first, last)

    returned = exchange(result, WIDE)
    mixed = combine(mix, returned.reshape(blocks * slots, width), planes)
    mixed = exchange(mixed, "far")
    return jnp.sum(mixed.astype(F32), axis=0).astype(BF)


def solution(mesh):
    torus = Mesh(
        mesh.devices.reshape(mesh.shape["expert"], 8, 2, 2), ("expert", "far", "near", "core")
    )
    placed = (
        P("expert", TENSOR),
        P("expert", None),
        P("expert", None),
        P("expert", TENSOR, None),
        P("expert", TENSOR, None),
        P("expert", TENSOR, None),
    )
    return jax.shard_map(
        local, mesh=torus, in_specs=placed, out_specs=P("expert", TENSOR), check_vma=False
    )
```

```python
import jax
import jax.numpy as jnp
from jax import lax
from jax.experimental import pallas as pl
from jax.experimental.pallas import tpu as pltpu
from jax.sharding import Mesh
from jax.sharding import PartitionSpec as P

BF = jnp.bfloat16
F32 = jnp.float32
TENSOR = ("far", "near", "core")
WIDE = ("expert", "near", "core")
ANY = pl.BlockSpec(memory_space=pl.ANY)
VMEM = pl.BlockSpec(memory_space=pltpu.VMEM)


def params(mib):
    return pltpu.CompilerParams(vmem_limit_bytes=mib * 2**20)


def dispatch(select, gathered, experts, cores):
    planes, rows, lanes = gathered.shape
    slots = select.shape[0] // experts // cores
    width = planes * lanes
    per = 4
    steps = planes // per

    def kernel(s_ref, x_ref, o_ref, held, sem):
        s = s_ref[...]
        copies = []
        for k in range(steps):
            x = jnp.concatenate([x_ref[per * k + i] for i in range(per)], axis=1)
            y = jnp.dot(s, x, preferred_element_type=F32).astype(BF)
            held[k] = y.reshape(experts, cores, slots, per * lanes)
            for i in range(4):
                at = pl.ds(k * per * lanes, per * lanes)
                out = o_ref.at[:, i // 2, i % 2, :, :, at]
                copies.append(pltpu.make_async_copy(held.at[k], out, sem.at[k, i]))
                copies[-1].start()
        for copy in copies:
            copy.wait()

    return pl.pallas_call(
        kernel,
        in_specs=[VMEM] * 2,
        out_specs=ANY,
        out_shape=jax.ShapeDtypeStruct((experts, 2, 2, cores, slots, width), BF),
        scratch_shapes=[
            pltpu.VMEM((steps, experts, cores, slots, per * lanes), BF),
            pltpu.SemaphoreType.DMA((steps, 4)),
        ],
        compiler_params=params(52),
        name="dispatch",
    )(select, gathered)


def stack_weights(own, other):
    units, features = own[0].shape
    tall = -(-units // 16) * 16
    span = features // 4

    def kernel(g, u, d, og, ou, od, out_ref):
        blank = jnp.zeros((tall - units, span), BF)
        for i, src in enumerate((g, og, u, ou, d, od)):
            out_ref[i * tall : (i + 1) * tall] = jnp.concatenate([src[...], blank], axis=0)

    def columns(rows):
        return pl.BlockSpec((rows, span), lambda i: (0, i))

    return pl.pallas_call(
        kernel,
        grid=(4,),
        in_specs=[columns(units)] * 6,
        out_specs=columns(6 * tall),
        out_shape=jax.ShapeDtypeStruct((6 * tall, features), BF),
        compiler_params=params(56),
        name="stack_weights",
        cost_estimate=pl.CostEstimate(
            flops=0, bytes_accessed=24 * units * features, transcendentals=0
        ),
    )(*own, *other)


def feed_forward(incoming, stacks, after):
    blocks, slots, width = incoming.shape
    tall, features = stacks.shape[0] // 3, stacks.shape[1]
    ways = features // width
    groups = blocks // ways
    rows = groups * slots
    steps = 4
    lanes = width // steps
    span = lanes * ways
    parts = lanes // 128
    halves = 2

    def kernel(x_ref, w_ref, _, o_ref, ws, ds, total, hidden, sw, sd):
        loads = []
        for t in range(steps):
            at = pl.ds(t * span, span)
            first = w_ref.at[pl.ds(0, 2 * tall), at]
            loads.append(pltpu.make_async_copy(first, ws.at[t], sw.at[t]))
        for t in range(halves):
            at = pl.ds(t * features // halves, features // halves)
            last = w_ref.at[pl.ds(2 * tall, tall), at]
            loads.append(pltpu.make_async_copy(last, ds.at[t], sd.at[t]))
        for load in loads:
            load.start()

        for t in range(steps):
            loads[t].wait()
            x = x_ref[:, :, t * lanes : (t + 1) * lanes].reshape(groups, ways, slots, lanes)
            x = jnp.concatenate(
                [
                    x[:, k, :, p * 128 : (p + 1) * 128].reshape(rows, 128)
                    for p in range(parts)
                    for k in range(ways)
                ],
                axis=1,
            )
            part = lax.dot_general(
                x, ws[t], (((1,), (1,)), ((), ())), preferred_element_type=F32
            )
            if t == 0:
                total[...] = part
            else:
                total[...] += part
        gate, up = total[:, :tall], total[:, tall:]
        hidden[...] = (gate / (1.0 + jnp.exp(-gate)) * up).astype(BF)

        for t in range(halves):
            loads[steps + t].wait()
            y = jnp.dot(hidden[...], ds[t], preferred_element_type=F32).astype(BF)
            for p in range(width // halves // 128):
                for k in range(ways):
                    at = (p * ways + k) * 128
                    to = t * width // halves + p * 128
                    o_ref[:, k, :, to : to + 128] = y[:, at : at + 128].reshape(groups, slots, 128)

    out = pl.pallas_call(
        kernel,
        in_specs=[VMEM, ANY, ANY],
        out_specs=VMEM,
        out_shape=jax.ShapeDtypeStruct((groups, ways, slots, width), BF),
        scratch_shapes=[
            pltpu.VMEM((steps, 2 * tall, span), BF),
            pltpu.VMEM((halves, tall, features // halves), BF),
            pltpu.VMEM((rows, 2 * tall), F32),
            pltpu.VMEM((rows, tall), BF),
            pltpu.SemaphoreType.DMA((steps,)),
            pltpu.SemaphoreType.DMA((halves,)),
        ],
        compiler_params=params(46),
        name="feed_forward",
    )(incoming, stacks, after)
    return out.reshape(blocks, slots, width)


def combine(weights, returned, planes):
    twice = weights.shape[0]
    rows = twice // 2
    lanes = returned.shape[1] // planes

    def kernel(w_ref, r_ref, o_ref):
        w = w_ref[...]
        for k in range(0, planes, 2):
            total = jnp.dot(w, r_ref[:, k * lanes : (k + 2) * lanes], preferred_element_type=F32)
            total = (total[:rows] + total[rows:]).astype(BF)
            o_ref[k] = total[:, :lanes]
            o_ref[k + 1] = total[:, lanes:]

    return pl.pallas_call(
        kernel,
        in_specs=[VMEM] * 2,
        out_specs=VMEM,
        out_shape=jax.ShapeDtypeStruct((planes, rows, lanes), BF),
        compiler_params=params(8),
        name="combine",
    )(weights, returned)


def slot_positions(route_block, experts, capacity):
    flat_routes = route_block.reshape(-1)
    onehot = (flat_routes[:, None] == jnp.arange(experts, dtype=jnp.int32)[None, :]).astype(
        jnp.int32
    )
    earlier = jnp.cumsum(onehot, axis=0) - onehot
    slot_index = jnp.sum(earlier * onehot, axis=1)
    return (flat_routes * capacity + slot_index).reshape(route_block.shape)


def exchange(blocks, axes):
    return lax.all_to_all(blocks, axes, split_axis=0, concat_axis=0, tiled=True)


def local(tokens, routes, route_weight, gate_weight, up_weight, down_weight):
    group_count = lax.axis_size("expert")
    planes = lax.axis_size("far")
    cores = lax.axis_size("core")
    experts = group_count // 2
    tok_rows, lanes = tokens.shape
    capacity = min(tok_rows, 4 * tok_rows // experts)
    slots_out = experts * capacity
    slots = capacity // cores
    blocks = group_count * 2 * cores
    width = planes * lanes

    gathered = exchange(jnp.broadcast_to(tokens[None], (planes, tok_rows, lanes)), "far")

    positions = slot_positions(routes, experts, capacity)
    slot_ids = jnp.arange(slots_out, dtype=jnp.int32)
    matches = positions[:, :, None] == slot_ids[None, None, :]
    select = jnp.any(matches, axis=1).astype(BF).T
    mix = jnp.sum(jnp.where(matches, route_weight[:, :, None], 0.0), axis=1)
    mix = mix.reshape(tok_rows, experts, 1, capacity)
    mix = jnp.broadcast_to(mix, (tok_rows, experts, 4, capacity)).reshape(tok_rows, 4 * slots_out)
    high = lax.reduce_precision(mix, 8, 7)
    mix = jnp.concatenate([high, mix - high], axis=0).astype(BF)

    outgoing = dispatch(select, gathered, experts, cores)
    own = (gate_weight[0], up_weight[0], down_weight[0])
    other = tuple(lax.ppermute(w, "core", [(0, 1), (1, 0)]) for w in own)
    incoming = exchange(outgoing.reshape(blocks, slots, width), WIDE)
    stacks = stack_weights(own, other)

    result = feed_forward(incoming, stacks, mix)

    returned = exchange(result, WIDE)
    mixed = combine(mix, returned.reshape(blocks * slots, width), planes)
    mixed = exchange(mixed, "far")
    return jnp.sum(mixed.astype(F32), axis=0).astype(BF)


def solution(mesh):
    torus = Mesh(
        mesh.devices.reshape(mesh.shape["expert"], 8, 2, 2), ("expert", "far", "near", "core")
    )
    placed = (
        P("expert", TENSOR),
        P("expert", None),
        P("expert", None),
        P("expert", TENSOR, None),
        P("expert", TENSOR, None),
        P("expert", TENSOR, None),
    )
    return jax.shard_map(
        local, mesh=torus, in_specs=placed, out_specs=P("expert", TENSOR), check_vma=False
    )
```

```python
import jax
import jax.numpy as jnp
from jax import lax
from jax.experimental import pallas as pl
from jax.experimental.pallas import tpu as pltpu
from jax.sharding import Mesh
from jax.sharding import PartitionSpec as P

BF = jnp.bfloat16
F32 = jnp.float32
TENSOR = ("far", "near", "core")
WIDE = ("expert", "near", "core")
ANY = pl.BlockSpec(memory_space=pl.ANY)
NT = (((1,), (1,)), ((), ()))
VMEM = pl.BlockSpec(memory_space=pltpu.VMEM)


def params(mib):
    return pltpu.CompilerParams(vmem_limit_bytes=mib * 2**20)


def dispatch(select, gathered, experts, cores):
    planes, rows, lanes = gathered.shape
    slots = select.shape[0] // experts // cores
    width = planes * lanes
    per = 4
    steps = planes // per

    def kernel(s_ref, x_ref, o_ref, held, sem):
        s = s_ref[...]
        copies = []
        for k in range(steps):
            x = jnp.concatenate([x_ref[per * k + i] for i in range(per)], axis=1)
            y = jnp.dot(s, x, preferred_element_type=F32).astype(BF)
            held[k] = y.reshape(experts, cores, slots, per * lanes)
            for i in range(4):
                at = pl.ds(k * per * lanes, per * lanes)
                out = o_ref.at[:, i // 2, i % 2, :, :, at]
                copies.append(pltpu.make_async_copy(held.at[k], out, sem.at[k, i]))
                copies[-1].start()
        for copy in copies:
            copy.wait()

    return pl.pallas_call(
        kernel,
        in_specs=[VMEM] * 2,
        out_specs=ANY,
        out_shape=jax.ShapeDtypeStruct((experts, 2, 2, cores, slots, width), BF),
        scratch_shapes=[
            pltpu.VMEM((steps, experts, cores, slots, per * lanes), BF),
            pltpu.SemaphoreType.DMA((steps, 4)),
        ],
        compiler_params=params(52),
        name="dispatch",
    )(select, gathered)


def stack_weights(own, other):
    units, features = own[0].shape
    tall = -(-units // 16) * 16
    span = features // 4

    def kernel(g, u, d, og, ou, od, out_ref):
        blank = jnp.zeros((tall - units, span), BF)
        for i, src in enumerate((g, og, u, ou, d, od)):
            out_ref[i * tall : (i + 1) * tall] = jnp.concatenate([src[...], blank], axis=0)

    def columns(rows):
        return pl.BlockSpec((rows, span), lambda i: (0, i))

    return pl.pallas_call(
        kernel,
        grid=(4,),
        in_specs=[columns(units)] * 6,
        out_specs=columns(6 * tall),
        out_shape=jax.ShapeDtypeStruct((6 * tall, features), BF),
        compiler_params=params(56),
        name="stack_weights",
        cost_estimate=pl.CostEstimate(
            flops=0, bytes_accessed=24 * units * features, transcendentals=0
        ),
    )(*own, *other)


def feed_forward(incoming, stacks, after):
    blocks, slots, width = incoming.shape
    tall, features = stacks.shape[0] // 3, stacks.shape[1]
    ways = features // width
    groups = blocks // ways
    rows = groups * slots
    steps = 4
    cuts = [width * n // 8 for n in (0, 2, 4, 7, 8)]
    halves = 2

    def kernel(x_ref, w_ref, _, o_ref, ws, ds, total, hidden, sw, sd):
        loads = []
        for t in range(steps):
            at = pl.ds(cuts[t] * ways, (cuts[t + 1] - cuts[t]) * ways)
            first = w_ref.at[pl.ds(0, 2 * tall), at]
            loads.append(pltpu.make_async_copy(first, ws.at[:, at], sw.at[t]))
        for t in range(halves):
            at = pl.ds(t * features // halves, features // halves)
            last = w_ref.at[pl.ds(2 * tall, tall), at]
            loads.append(pltpu.make_async_copy(last, ds.at[t], sd.at[t]))
        for load in loads:
            load.start()

        for t in range(steps):
            loads[t].wait()
            lanes = cuts[t + 1] - cuts[t]
            x = x_ref[:, :, cuts[t] : cuts[t + 1]].reshape(groups, ways, slots, lanes)
            x = jnp.concatenate(
                [
                    x[:, k, :, p * 128 : (p + 1) * 128].reshape(rows, 128)
                    for p in range(lanes // 128)
                    for k in range(ways)
                ],
                axis=1,
            )
            part = lax.dot_general(
                x, ws[:, cuts[t] * ways : cuts[t + 1] * ways], NT, preferred_element_type=F32
            )
            if t == 0:
                total[...] = part
            else:
                total[...] += part
        gate, up = total[:, :tall], total[:, tall:]
        hidden[...] = (gate / (1.0 + jnp.exp(-gate)) * up).astype(BF)

        for t in range(halves):
            loads[steps + t].wait()
            y = jnp.dot(hidden[...], ds[t], preferred_element_type=F32).astype(BF)
            for p in range(width // halves // 128):
                for k in range(ways):
                    at = (p * ways + k) * 128
                    to = t * width // halves + p * 128
                    o_ref[:, k, :, to : to + 128] = y[:, at : at + 128].reshape(groups, slots, 128)

    out = pl.pallas_call(
        kernel,
        in_specs=[VMEM, ANY, ANY],
        out_specs=VMEM,
        out_shape=jax.ShapeDtypeStruct((groups, ways, slots, width), BF),
        scratch_shapes=[
            pltpu.VMEM((2 * tall, features), BF),
            pltpu.VMEM((halves, tall, features // halves), BF),
            pltpu.VMEM((rows, 2 * tall), F32),
            pltpu.VMEM((rows, tall), BF),
            pltpu.SemaphoreType.DMA((steps,)),
            pltpu.SemaphoreType.DMA((halves,)),
        ],
        compiler_params=params(46),
        name="feed_forward",
    )(incoming, stacks, after)
    return out.reshape(blocks, slots, width)


def combine(weights, returned, planes):
    twice = weights.shape[0]
    rows = twice // 2
    lanes = returned.shape[1] // planes

    def kernel(w_ref, r_ref, o_ref):
        w = w_ref[...]
        for k in range(0, planes, 2):
            total = jnp.dot(w, r_ref[:, k * lanes : (k + 2) * lanes], preferred_element_type=F32)
            total = (total[:rows] + total[rows:]).astype(BF)
            o_ref[k] = total[:, :lanes]
            o_ref[k + 1] = total[:, lanes:]

    return pl.pallas_call(
        kernel,
        in_specs=[VMEM] * 2,
        out_specs=VMEM,
        out_shape=jax.ShapeDtypeStruct((planes, rows, lanes), BF),
        compiler_params=params(8),
        name="combine",
    )(weights, returned)


def slot_positions(route_block, experts, capacity):
    flat_routes = route_block.reshape(-1)
    onehot = (flat_routes[:, None] == jnp.arange(experts, dtype=jnp.int32)[None, :]).astype(
        jnp.int32
    )
    earlier = jnp.cumsum(onehot, axis=0) - onehot
    slot_index = jnp.sum(earlier * onehot, axis=1)
    return (flat_routes * capacity + slot_index).reshape(route_block.shape)


def exchange(blocks, axes):
    return lax.all_to_all(blocks, axes, split_axis=0, concat_axis=0, tiled=True)


def local(tokens, routes, route_weight, gate_weight, up_weight, down_weight):
    group_count = lax.axis_size("expert")
    planes = lax.axis_size("far")
    cores = lax.axis_size("core")
    experts = group_count // 2
    tok_rows, lanes = tokens.shape
    capacity = min(tok_rows, 4 * tok_rows // experts)
    slots_out = experts * capacity
    slots = capacity // cores
    blocks = group_count * 2 * cores
    width = planes * lanes

    gathered = exchange(jnp.broadcast_to(tokens[None], (planes, tok_rows, lanes)), "far")

    positions = slot_positions(routes, experts, capacity)
    slot_ids = jnp.arange(slots_out, dtype=jnp.int32)
    matches = positions[:, :, None] == slot_ids[None, None, :]
    select = jnp.any(matches, axis=1).astype(BF).T
    mix = jnp.sum(jnp.where(matches, route_weight[:, :, None], 0.0), axis=1)
    mix = mix.reshape(tok_rows, experts, 1, capacity)
    mix = jnp.broadcast_to(mix, (tok_rows, experts, 4, capacity)).reshape(tok_rows, 4 * slots_out)
    high = lax.reduce_precision(mix, 8, 7)
    mix = jnp.concatenate([high, mix - high], axis=0).astype(BF)

    outgoing = dispatch(select, gathered, experts, cores)
    own = (gate_weight[0], up_weight[0], down_weight[0])
    other = tuple(lax.ppermute(w, "core", [(0, 1), (1, 0)]) for w in own)
    incoming = exchange(outgoing.reshape(blocks, slots, width), WIDE)
    stacks = stack_weights(own, other)

    result = feed_forward(incoming, stacks, mix)

    returned = exchange(result, WIDE)
    mixed = combine(mix, returned.reshape(blocks * slots, width), planes)
    mixed = exchange(mixed, "far")
    return jnp.sum(mixed.astype(F32), axis=0).astype(BF)


def solution(mesh):
    torus = Mesh(
        mesh.devices.reshape(mesh.shape["expert"], 8, 2, 2), ("expert", "far", "near", "core")
    )
    placed = (
        P("expert", TENSOR),
        P("expert", None),
        P("expert", None),
        P("expert", TENSOR, None),
        P("expert", TENSOR, None),
        P("expert", TENSOR, None),
    )
    return jax.shard_map(
        local, mesh=torus, in_specs=placed, out_specs=P("expert", TENSOR), check_vma=False
    )
```
